32 devices in a mesh: ulysses: 4 (over x, core), context: 8 (over z, y).
Axes of the slice: x: 2, y: 2, z: 4, core: 2. Of those that a mesh axis runs over, the one named last changes fastest.
Arguments:
- queries: bfloat16 [4096, 2048], P(('context', 'ulysses')), may hold values from -6 to 6
- key_rows: bfloat16 [4096, 2048], P(('context', 'ulysses')), may hold values from -6 to 6
- value_rows: bfloat16 [4096, 2048], P(('context', 'ulysses')), may hold values from -6 to 6
- grad_out: bfloat16 [4096, 2048], P(('context', 'ulysses')), may hold values from -6 to 6
Outputs:
- attended: bfloat16 [4096, 2048], P(('context', 'ulysses'))
- grad_queries: bfloat16 [4096, 2048], P(('context', 'ulysses'))
- grad_keys: bfloat16 [4096, 2048], P(('context', 'ulysses'))
- grad_values: bfloat16 [4096, 2048], P(('context', 'ulysses'))
The draws below stay inside these ranges and needn't reach their ends.
All inputs are finite; a program needn't handle non-finite values.
Results may differ from the reference program's by a relative error of at most 0.03.
Values may be sent and summed in bfloat16 or wider, within the bound.
No kernel may reach another device: no remote copies, remote signals or barrier semaphores. Data moves between devices by JAX's collectives and lax.ppermute only.
A program may use at most 128 MiB of HBM per device.

```python
import jax
import jax.numpy as jnp
from jax import lax

HEADS = 16
HEAD_DIM = 128
D = 2048
BLOCK = 512
LEVELS = 3
TOKENS = 4096


def drawn_pair(key):
    base_key = jax.random.fold_in(key, 7)
    query_part = jnp.clip(jax.random.normal(jax.random.fold_in(base_key, 1), (TOKENS, D), jnp.float32), -6.0, 6.0)
    key_part = jnp.clip(jax.random.normal(jax.random.fold_in(base_key, 2), (TOKENS, D), jnp.float32), -6.0, 6.0)
    return (query_part, key_part)


def draw_queries(key, part):
    return drawn_pair(key)[0].astype(jnp.bfloat16)


def draw_key_rows(key, part):
    return drawn_pair(key)[1].astype(jnp.bfloat16)


def level_of(own_key, dims, shards, least, high):
    def one(axis_at, parts):
        draws = jax.random.uniform(jax.random.fold_in(jax.random.fold_in(own_key, 6), axis_at), (parts,), jnp.float32, least / len(shards), high / len(shards))
        return jnp.repeat(jnp.exp(draws), dims[axis_at] // parts).reshape((-1,) + (1,) * (len(dims) - axis_at - 1))

    level = one(*shards[0])
    for cut in shards[1:]:
        level = level * one(*cut)
    return level


def scatter_about(key, shape, spread, reach, split=(), kind=jnp.bfloat16):
    gain = level_of(key, shape, split, -0.22, 0.18) if split else 1.0
    drawn = jax.random.normal(key, shape, jnp.float32) * spread * gain
    return jnp.minimum(jnp.maximum(drawn, -reach), reach).astype(kind)


def setup_inputs(seed: int = 0) -> dict:
    seeds = jax.random.split(jax.random.key(seed), 5)
    return {
        "queries": draw_queries(jax.random.fold_in(seeds[4], 71), 0),
        "key_rows": draw_key_rows(jax.random.fold_in(seeds[4], 71), 0),
        "value_rows": scatter_about(seeds[2], (TOKENS, D), 1.0, 6.0, ((0, 32),)),
        "grad_out": scatter_about(seeds[3], (TOKENS, D), 1.0, 6.0, ((0, 32),)),
    }


def rounded_values(values_in):
    return lax.optimization_barrier(values_in.astype(jnp.bfloat16)).astype(jnp.float32)


def one_head(head_args, partner):
    query_h, key_h, value_h, grad_h = head_args
    softmax_scale = HEAD_DIM ** -0.5
    query_full = query_h.astype(jnp.float32)
    gradient_full = grad_h.astype(jnp.float32)
    key_groups = key_h[partner].astype(jnp.float32)
    value_groups = value_h[partner].astype(jnp.float32)
    logit_scores = jnp.einsum("hpe,hwye->hwpy", query_full, key_groups) * softmax_scale
    block_peak = jnp.max(logit_scores, axis=-1)
    shifted = jnp.exp(logit_scores - block_peak[..., None])
    block_total = jnp.sum(shifted, axis=-1)
    block_weights = rounded_values(shifted)
    block_out = jnp.einsum("bjqk,bjkd->bjqd", block_weights, value_groups)
    peak = jnp.max(block_peak, axis=1)
    factor = jnp.exp(block_peak - peak[:, None, :])
    norm = jnp.sum(factor * block_total, axis=1)
    attended = (jnp.sum(factor[..., None] * block_out, axis=1) / norm[..., None]).astype(jnp.bfloat16)
    log_norm = peak + jnp.log(norm)
    dot_term = jnp.sum(gradient_full * attended.astype(jnp.float32), axis=-1)
    probs = jnp.exp(logit_scores - log_norm[:, None, :, None])
    probabilities_reduced = rounded_values(probs)
    value_contributions = rounded_values(jnp.einsum("onhp,oha->onpa", probabilities_reduced, gradient_full))
    probability_gradient = jnp.einsum("hpe,hwye->hwpy", gradient_full, value_groups)
    score_gradient = rounded_values(probs * (probability_gradient - dot_term[:, None, :, None]) * softmax_scale)
    query_terms = rounded_values(jnp.einsum("bjqk,bjkd->bjqd", score_gradient, key_groups))
    key_contributions = rounded_values(jnp.einsum("onhp,oha->onpa", score_gradient, query_full))
    slot_index = jnp.arange(LEVELS + 1, dtype=jnp.int32)[None, :]
    grad_query = jnp.sum(query_terms, axis=1).astype(jnp.bfloat16)
    grad_key = jnp.sum(key_contributions[partner, slot_index], axis=1).astype(jnp.bfloat16)
    grad_value = jnp.sum(value_contributions[partner, slot_index], axis=1).astype(jnp.bfloat16)
    return attended, grad_query, grad_key, grad_value


def reference(queries, key_rows, value_rows, grad_out):
    nblocks = TOKENS // BLOCK

    def by_heads(array_in):
        return array_in.reshape(nblocks, BLOCK, HEADS, HEAD_DIM).transpose(2, 0, 1, 3)

    def by_tokens(array_in):
        return array_in.transpose(1, 2, 0, 3).reshape(TOKENS, D)

    block_ids = jnp.arange(nblocks, dtype=jnp.int32)
    distances = jnp.concatenate([jnp.zeros((1,), jnp.int32), jnp.left_shift(jnp.ones((LEVELS,), jnp.int32), jnp.arange(LEVELS, dtype=jnp.int32))])
    partner = jnp.bitwise_xor(block_ids[:, None], distances[None, :]).astype(jnp.int32)
    results = lax.map(lambda head_args: one_head(head_args, partner), (by_heads(queries), by_heads(key_rows), by_heads(value_rows), by_heads(grad_out)))
    return (by_tokens(results[0]), by_tokens(results[1]), by_tokens(results[2]), by_tokens(results[3]))
```

```python
import functools

import jax
import jax.numpy as jnp
from jax import lax
from jax.experimental import pallas as pl
from jax.experimental.pallas import tpu as pltpu
from jax.sharding import PartitionSpec as P

HEAD_DIM = 128
CHUNKS = 2
SCALE = HEAD_DIM ** (-0.5)
LOG2E = 1.4426950408889634

NT = (((1,), (1,)), ((), ()))
TN = (((0,), (0,)), ((), ()))
NN = (((1,), (0,)), ((), ()))


def dot(a, b, dims):
    return lax.dot_general(a, b, dims, preferred_element_type=jnp.float32)


def permuted(x, axis, distance):
    return lax.ppermute(x, axis, [(i, i ^ distance) for i in range(lax.axis_size(axis))])


def params():
    return pltpu.CompilerParams(vmem_limit_bytes=48 * 1024 * 1024)


def pack_kernel(members, chunks, me_ref, a_ref, b_ref, *outs):
    me = me_ref[0]
    width = a_ref.shape[1] // members
    part = width // chunks
    for c in range(chunks):
        for k in range(members):
            at = pl.multiple_of((me ^ k) * width + c * part, part)
            outs[c * members + k][0] = a_ref[:, pl.ds(at, part)]
            outs[c * members + k][1] = b_ref[:, pl.ds(at, part)]


def pack(me, a, b, members, chunks):
    tokens, features = a.shape
    piece = jax.ShapeDtypeStruct((2, tokens, features // members // chunks), a.dtype)
    outs = pl.pallas_call(
        functools.partial(pack_kernel, members, chunks),
        out_shape=[piece] * (chunks * members),
        in_specs=[
            pl.BlockSpec(memory_space=pltpu.SMEM),
            pl.BlockSpec(memory_space=pltpu.VMEM),
            pl.BlockSpec(memory_space=pltpu.VMEM),
        ],
        out_specs=[pl.BlockSpec(memory_space=pltpu.VMEM)] * (chunks * members),
        compiler_params=params(),
        cost_estimate=pl.CostEstimate(flops=0, bytes_accessed=4 * a.size * 2, transcendentals=0),
        name="pack",
    )(me, a, b)
    return [outs[c * members : (c + 1) * members] for c in range(chunks)]


def unpack_kernel(members, chunks, me_ref, *refs):
    pieces, (a_ref, b_ref) = refs[:-2], refs[-2:]
    me = me_ref[0]
    width = a_ref.shape[1] // members
    part = width // chunks
    for c in range(chunks):
        for k in range(members):
            at = pl.multiple_of((me ^ k) * width + c * part, part)
            a_ref[:, pl.ds(at, part)] = pieces[c * members + k][0]
            b_ref[:, pl.ds(at, part)] = pieces[c * members + k][1]


def unpack(me, pieces, members, chunks):
    tokens, part = pieces[0].shape[1:]
    whole = jax.ShapeDtypeStruct((tokens, part * members * chunks), pieces[0].dtype)
    return pl.pallas_call(
        functools.partial(unpack_kernel, members, chunks),
        out_shape=[whole] * 2,
        in_specs=[pl.BlockSpec(memory_space=pltpu.SMEM)]
        + [pl.BlockSpec(memory_space=pltpu.VMEM)] * len(pieces),
        out_specs=[pl.BlockSpec(memory_space=pltpu.VMEM)] * 2,
        compiler_params=params(),
        cost_estimate=pl.CostEstimate(
            flops=0, bytes_accessed=4 * tokens * part * members * chunks * 2, transcendentals=0
        ),
        name="unpack",
    )(me, *pieces)


def forward_block(query, key, value, state):
    raw = dot(key, query, NT)
    top = jnp.max(raw, axis=0, keepdims=True) * (SCALE * LOG2E)
    if state is not None:
        old_top, old_total, old_out = state
        top = jnp.maximum(top, old_top)
    weights = jnp.exp2(raw * (SCALE * LOG2E) - top)
    total = jnp.sum(weights, axis=0, keepdims=True)
    out = dot(value, weights.astype(jnp.bfloat16), TN)
    if state is not None:
        factor = jnp.exp2(old_top - top)
        total = total + old_total * factor
        out = out + old_out * factor
    return raw, (top, total, out)


def backward_block(query, grad, key, value, log_norm, dot_term, raw=None):
    if raw is None:
        raw = dot(key, query, NT)
    probs = jnp.exp2(raw * (SCALE * LOG2E) - log_norm)
    value_term = dot(probs.astype(jnp.bfloat16), grad, NN)
    grad_probs = dot(value, grad, NT)
    grad_scores = (probs * (grad_probs - dot_term)).astype(jnp.bfloat16)
    key_term = dot(grad_scores, query, NN) * SCALE
    query_term = dot(key, grad_scores, TN) * SCALE
    return key_term.astype(jnp.bfloat16), value_term.astype(jnp.bfloat16), query_term


def first_kernel(blocks, *refs):
    qg_ref, kv_refs = refs[0], refs[1 : 1 + blocks]
    top_ref, total_ref, out_ref = refs[1 + blocks :]
    query = qg_ref[0]
    state = None
    for kv in kv_refs:
        _, state = forward_block(query, kv[0], kv[1], state)
    top_ref[0], total_ref[0], out_ref[0] = state


def middle_kernel(qg_ref, kv_ref, top_ref, total_ref, out_ref, o_ref, norm_ref, dot_ref, dq_ref, term_ref):
    query, grad = qg_ref[0], qg_ref[1]
    key, value = kv_ref[0], kv_ref[1]
    raw, (top, total, out) = forward_block(query, key, value, (top_ref[0], total_ref[0], out_ref[0]))
    attended = (out / total).astype(jnp.bfloat16)
    o_ref[...] = attended.T
    log_norm = top + jnp.log2(total)
    dot_term = jnp.sum(attended.astype(jnp.float32) * grad.T.astype(jnp.float32), axis=0, keepdims=True)
    norm_ref[0] = log_norm
    dot_ref[0] = dot_term
    term_ref[0], term_ref[1], dq_ref[0] = backward_block(query, grad, key, value, log_norm, dot_term, raw)


def last_kernel(blocks, members, *refs):
    qg_ref, norm_ref, dot_ref, dq_ref, o_ref = refs[:5]
    kv_refs = refs[5 : 5 + blocks]
    term_refs = refs[5 + blocks : 5 + 2 * blocks]
    piece_refs = refs[5 + 2 * blocks :]
    query, grad = qg_ref[0], qg_ref[1]
    total = dq_ref[0]
    for kv, term in zip(reversed(kv_refs), reversed(term_refs)):
        term[0], term[1], more = backward_block(query, grad, kv[0], kv[1], norm_ref[0], dot_ref[0])
        total = total + more
    grad_query = total.T.astype(jnp.bfloat16)
    rows = grad_query.shape[0] // members
    for k in range(members):
        piece_refs[k][0] = o_ref[k * rows : (k + 1) * rows, :]
        piece_refs[k][1] = grad_query[k * rows : (k + 1) * rows, :]


def cost(products, block, heads):
    return pl.CostEstimate(
        flops=2 * products * heads * block * block * HEAD_DIM,
        bytes_accessed=products * heads * block * HEAD_DIM * 2,
        transcendentals=products * heads * block * block // 3,
    )


def attend(qg, kvs, members):
    _, block, width = qg.shape
    heads = width // HEAD_DIM
    pair = pl.BlockSpec((2, block, HEAD_DIM), lambda h: (0, 0, h))
    row = pl.BlockSpec((1, 1, block), lambda h: (h, 0, 0))
    turned = pl.BlockSpec((1, HEAD_DIM, block), lambda h: (h, 0, 0))
    flat = pl.BlockSpec((block, HEAD_DIM), lambda h: (0, h))
    row_shape = jax.ShapeDtypeStruct((heads, 1, block), jnp.float32)
    turned_shape = jax.ShapeDtypeStruct((heads, HEAD_DIM, block), jnp.float32)
    flat_shape = jax.ShapeDtypeStruct((block, width), jnp.bfloat16)
    early, late = kvs[:-1], kvs[-1]
    blocks = len(early)
    top, total, out = pl.pallas_call(
        functools.partial(first_kernel, blocks),
        grid=(heads,),
        out_shape=[row_shape, row_shape, turned_shape],
        in_specs=[pair] * (1 + blocks),
        out_specs=[row, row, turned],
        compiler_params=params(),
        cost_estimate=cost(2 * blocks, block, heads),
        name="first",
    )(qg, *early)
    attended, log_norm, dot_term, grad_query, late_term = pl.pallas_call(
        middle_kernel,
        grid=(heads,),
        out_shape=[flat_shape, row_shape, row_shape, turned_shape, jax.ShapeDtypeStruct(late.shape, jnp.bfloat16)],
        in_specs=[pair, pair, row, row, turned],
        out_specs=[flat, row, row, turned, pair],
        compiler_params=params(),
        cost_estimate=cost(6, block, heads),
        name="middle",
    )(qg, late, top, total, out)
    piece = pl.BlockSpec((2, block // members, HEAD_DIM), lambda h: (0, 0, h))
    results = pl.pallas_call(
        functools.partial(last_kernel, blocks, members),
        grid=(heads,),
        out_shape=[jax.ShapeDtypeStruct(late.shape, jnp.bfloat16)] * blocks
        + [jax.ShapeDtypeStruct((2, block // members, width), jnp.bfloat16)] * members,
        in_specs=[pair, row, row, turned, flat] + [pair] * blocks,
        out_specs=[pair] * blocks + [piece] * members,
        compiler_params=params(),
        cost_estimate=cost(5 * blocks, block, heads),
        name="last",
    )(qg, log_norm, dot_term, grad_query, attended, *early)
    return list(results[:blocks]) + [late_term], list(results[blocks:])


def finish_kernel(members, *refs):
    terms, outs = refs[: len(refs) - members], refs[len(refs) - members :]
    rows = outs[0].shape[1]
    for k in range(members):
        total = terms[0][:, k * rows : (k + 1) * rows, :].astype(jnp.float32)
        for term in terms[1:]:
            total = total + term[:, k * rows : (k + 1) * rows, :].astype(jnp.float32)
        outs[k][...] = total.astype(jnp.bfloat16)


def finish(terms, members):
    two, block, width = terms[0].shape
    vmem = pl.BlockSpec(memory_space=pltpu.VMEM)
    return pl.pallas_call(
        functools.partial(finish_kernel, members),
        out_shape=[jax.ShapeDtypeStruct((two, block // members, width), jnp.bfloat16)] * members,
        in_specs=[vmem] * len(terms),
        out_specs=[vmem] * members,
        compiler_params=params(),
        cost_estimate=pl.CostEstimate(
            flops=terms[0].size * len(terms), bytes_accessed=2 * terms[0].size * (len(terms) + 1), transcendentals=0
        ),
        name="finish",
    )(*terms)


def exchange(pieces):
    return [pieces[0]] + [permuted(piece, "ulysses", k) for k, piece in enumerate(pieces) if k]


def body(queries, key_rows, value_rows, grad_out):
    members = lax.axis_size("ulysses")
    levels = lax.axis_size("context").bit_length() - 1
    me = lax.axis_index("ulysses").astype(jnp.int32).reshape(1)
    tokens, features = queries.shape
    block = tokens * members
    kv_pieces = pack(me, key_rows, value_rows, members, CHUNKS)
    qg_pieces = pack(me, queries, grad_out, members, CHUNKS)

    def joined(pieces):
        return jnp.stack(pieces, axis=1).reshape(2, block, pieces[0].shape[2])

    kv_got = [exchange(p) for p in kv_pieces]
    qg_got = [exchange(p) for p in qg_pieces]
    state = []
    for c in range(CHUNKS):
        own = joined(kv_got[c])
        kvs = [own]
        for level in range(levels):
            if level and level % 2 == 0:
                kvs.append(permuted(kvs[-1], "context", 3 << (level - 1)))
            else:
                kvs.append(permuted(own, "context", 1 << level))
        state.append((joined(qg_got[c]), kvs))
    out_pieces, grad_pieces = [], []
    for c in range(CHUNKS):
        qg, kvs = state[c]
        terms, pieces = attend(qg, kvs, members)
        out_pieces += exchange(pieces)
        gathered = [terms[0]]
        carried = None
        for level in reversed(range(levels)):
            term = terms[level + 1]
            if carried is not None:
                term = (term.astype(jnp.float32) + carried.astype(jnp.float32)).astype(jnp.bfloat16)
                carried = None
            if level and level % 2 == 0:
                carried = permuted(term, "context", 3 << (level - 1))
            else:
                gathered.append(permuted(term, "context", 1 << level))
        grad_pieces += exchange(finish(gathered, members))
    attended, grad_query = unpack(me, out_pieces, members, CHUNKS)
    grad_key, grad_value = unpack(me, grad_pieces, members, CHUNKS)
    return attended, grad_query, grad_key, grad_value


def solution(mesh):
    placed = P(("context", "ulysses"), None)
    return jax.shard_map(
        body, mesh=mesh, in_specs=(placed,) * 4, out_specs=(placed,) * 4, check_vma=False
    )
```
